256 devices in a mesh: grp: 8 (over z_hi, core), mem: 32 (over y, x, z_lo).
Axes of the slice: x: 4, y: 4, z: 8 (z_hi: 4, z_lo: 2; z = z_hi * 2 + z_lo), core: 2. Of those that a mesh axis runs over, the one named last changes fastest.
Arguments:
- spectra: bfloat16 [3072, 64, 384], P(('grp', 'mem')), may hold values from -45 to 45
Outputs:
- correlations: bfloat16 [7, 8, 384, 32, 12, 128], P(None, 'grp', None, 'mem')
The draws below stay inside these ranges and needn't reach their ends.
All inputs are finite; a program needn't handle non-finite values.
Results may differ from the reference program's by a relative error of at most 0.0067.
Values may be sent and summed in bfloat16 or wider, within the bound.
No kernel may reach another device: no remote copies, remote signals or barrier semaphores. Data moves between devices by JAX's collectives and lax.ppermute only.
A program may use at most 128 MiB of HBM per device.

```python
import math
import jax
import jax.numpy as jnp
from jax import lax

F = 64
W = 192
CH_DEV = 12
LAGS = 128
GCH = 384
CHANNELS = 3072
ROUNDS = 7
N_GRP = 8
N_MEM = 32


def draw_spectra(key, part):
    keys = jax.random.split(key, 3)
    shape = (CHANNELS, F, 2 * W)
    base = jax.random.normal(keys[0], shape, jnp.float32)
    base = jnp.clip(base, -4.0, 4.0)
    bin_scale = jnp.exp(jax.random.uniform(keys[1], (CHANNELS, F, 1), jnp.float32, -1.2, 1.2))
    window_scale = jnp.exp(jax.random.uniform(keys[2], (CHANNELS, 1, W), jnp.float32, -1.2, 1.2))
    window_scale = jnp.concatenate([window_scale, window_scale], -1)
    return (base * bin_scale * window_scale).astype(jnp.bfloat16)


def setup_inputs(seed: int = 0) -> dict:
    splits = jax.random.split(jax.random.key(seed), 2)
    spectra = draw_spectra(jax.random.fold_in(splits[1], 71), 0)
    return dict(spectra=spectra)


def whiten(spectra):
    values = spectra.astype(jnp.float32)
    windows = values.shape[-1] // 2
    power_sum = values[..., :windows] ** 2 + values[..., windows:] ** 2
    amplitude = jnp.sqrt(lax.optimization_barrier(jnp.mean(power_sum, axis=1, keepdims=True)) + 1e-06)
    divisor = jnp.concatenate([amplitude, amplitude], -1)
    return (values / divisor).astype(jnp.bfloat16)

def lag_table(bin_count, lag_count):
    freq_index = jnp.arange(bin_count, dtype=jnp.int32)
    lag_index = jnp.arange(lag_count, dtype=jnp.int32)
    product = freq_index[:, None] * lag_index[None, :] % lag_count
    phase = product.astype(jnp.float32) * (2.0 * math.pi / lag_count)
    weight = 1.0 / math.sqrt(bin_count)
    return (jnp.stack([jnp.cos(phase), -jnp.sin(phase)]) * weight).astype(jnp.bfloat16)

def round_partners(group_count):
    last_label = group_count - 1
    round_label = jnp.arange(last_label, dtype=jnp.int32)[:, None]
    label_index = jnp.arange(group_count, dtype=jnp.int32)[None, :]
    opposite = jnp.mod(2 * round_label - label_index, last_label)
    inner = jnp.where(opposite == label_index, last_label, opposite)
    return jnp.where(label_index == last_label, round_label, inner).astype(jnp.int32)

def reference(spectra):
    white = whiten(spectra)
    pairing = round_partners(N_GRP)
    groups = white.reshape(N_GRP, GCH, F, 2 * W)
    blocks = white.reshape(N_GRP, N_MEM, CH_DEV, F, 2 * W)
    flat_table = lag_table(F, LAGS).reshape(2 * F, LAGS).astype(jnp.float32)
    norm_scale = 1.0 / math.sqrt(W)

    def per_round(round_index):

        def per_group(group_index):
            partner = pairing[round_index, group_index].astype(jnp.int32)
            partner_blocks = lax.dynamic_index_in_dim(blocks, partner, 0, keepdims=False)
            rotated = jnp.concatenate([-partner_blocks[..., W:], partner_blocks[..., :W]], -1)
            stacked = jnp.stack([partner_blocks, rotated], 2)
            own_rows = lax.dynamic_index_in_dim(groups, group_index, 0, keepdims=False)
            spectrum = jnp.einsum('nfw,mdsfw->nmdsf', own_rows.astype(jnp.float32), stacked.astype(jnp.float32)) * norm_scale
            spectrum = spectrum.astype(jnp.bfloat16).reshape(GCH, N_MEM, CH_DEV, 2 * F)
            correlated = jnp.einsum('nmdx,xl->nmdl', spectrum.astype(jnp.float32), flat_table)
            return correlated.astype(jnp.bfloat16)
        return lax.map(per_group, jnp.arange(N_GRP, dtype=jnp.int32))
    return lax.map(per_round, jnp.arange(ROUNDS, dtype=jnp.int32))
```

```python
import functools
import math

import jax
import jax.numpy as jnp
from jax import lax
from jax.experimental import pallas as pl
from jax.experimental.pallas import tpu as pltpu
from jax.sharding import Mesh, PartitionSpec as P


BF = jnp.bfloat16
F32 = jnp.float32
F, W, CH, LAGS = 64, 192, 12, 128
W2 = 2 * W
ROWS = F * CH
ROUNDS = 7
FG = 4
GROUP = FG * CH
UNITS = 16
STACK = ROUNDS * 2 * CH


def whiten_kernel(x_ref, o_ref, t_ref):
    for c in range(CH):
        v = x_ref[c].astype(F32)
        total = jnp.sum(v * v, axis=0, keepdims=True)
        mean = (total[:, :W] + total[:, W:]) * (1.0 / F)
        amplitude = jnp.sqrt(mean + 1e-06)
        divisor = jnp.concatenate([amplitude, amplitude], 1)
        q = v / divisor
        for j in range(3):
            t_ref[j, pl.ds(c, F, stride=CH), :] = q[:, 128 * j : 128 * j + 128]
    for j in range(3):
        o_ref[:, 128 * j : 128 * j + 128] = t_ref[j].astype(BF)


def whiten(spectra):
    return pl.pallas_call(
        whiten_kernel,
        out_shape=jax.ShapeDtypeStruct((ROWS, W2), BF),
        scratch_shapes=[pltpu.VMEM((3, ROWS, 128), F32)],
        cost_estimate=pl.CostEstimate(
            flops=6 * ROWS * W2, bytes_accessed=4 * ROWS * W2, transcendentals=0
        ),
        name="whiten",
    )(spectra)


def stack_kernel(*refs):
    o_ref = refs[-1]
    plain, turned = [], []
    for ref in refs[:-1]:
        v = ref[...].astype(F32)
        plain.append(v)
        turned.append(jnp.concatenate([-v[:, W:], v[:, :W]], 1))
    for j in range(FG):
        rows = slice(CH * j, CH * j + CH)
        parts = []
        for v, t in zip(plain, turned):
            parts += [v[rows], t[rows]]
        o_ref[j] = jnp.concatenate(parts, 0).astype(BF)


def make_stack(blocks):
    return pl.pallas_call(
        stack_kernel,
        grid=(F // FG,),
        in_specs=[pl.BlockSpec((GROUP, W2), lambda i: (i, 0))] * ROUNDS,
        out_specs=pl.BlockSpec((FG, STACK, W2), lambda i: (i, 0, 0)),
        out_shape=jax.ShapeDtypeStruct((F, STACK, W2), BF),
        cost_estimate=pl.CostEstimate(
            flops=2 * F * STACK * W2,
            bytes_accessed=3 * F * STACK * W2,
            transcendentals=0,
        ),
        name="stack",
    )(*blocks)


def correlate_kernel(n_arr, aliased, scale, *refs):
    meta = refs[0]
    stack_ref, table_ref = refs[1], refs[2]
    row_refs = refs[3 : 3 + 2 * n_arr]
    at = 3 + 2 * n_arr + (1 if aliased else 0)
    out_ref, spec_ref, buf_ref, sem = refs[at : at + 4]
    units = 2 * n_arr
    lanes = 24 * units
    steps = F // FG
    i = pl.program_id(0)

    @pl.when(i < steps)
    def _():
        swap = meta[0] == 1
        firsts, seconds = [], []
        for a in range(n_arr):
            for b in range(2):
                u = row_refs[2 * a][b].astype(F32)
                v = row_refs[2 * a + 1][b].astype(F32)
                firsts.append(jnp.where(swap, v, u))
                seconds.append(jnp.where(swap, u, v))
        for j in range(FG):
            rows = slice(CH * j, CH * j + CH)
            parts = []
            for u, v in zip(firsts, seconds):
                parts += [u[rows], v[rows]]
            mat = jnp.concatenate(parts, 0).astype(BF)
            res = (
                lax.dot_general(
                    stack_ref[j],
                    mat,
                    (((1,), (1,)), ((), ())),
                    preferred_element_type=F32,
                )
                * scale
            )
            for k in range(0, lanes, 128):
                wide = min(128, lanes - k)
                spec_ref[k // 128, pl.ds(i * FG + j, STACK, stride=F), 0:wide] = res[
                    :, k : k + wide
                ]

    def copies(slot, buf):
        return [
            pltpu.make_async_copy(
                buf_ref.at[buf, :, k],
                out_ref.at[meta[1 + slot], :, meta[8 + k]],
                sem.at[buf, k],
            )
            for k in range(units)
        ]

    @pl.when(i >= steps)
    def _():
        slot = i - steps
        buf = lax.rem(slot, 2)

        @pl.when(slot >= 2)
        def _():
            for c in copies(slot - 2, buf):
                c.wait()

        table = table_ref[...]
        for d in range(CH):
            for k in range(0, lanes, 128):
                wide = min(128, lanes - k)
                re0 = pl.multiple_of((slot * 24 + d) * F, F)
                im0 = pl.multiple_of((slot * 24 + CH + d) * F, F)
                cross = jnp.concatenate(
                    [
                        spec_ref[k // 128, pl.ds(re0, F), :],
                        spec_ref[k // 128, pl.ds(im0, F), :],
                    ],
                    0,
                ).astype(BF)
                res = lax.dot_general(
                    cross,
                    table,
                    (((0,), (0,)), ((), ())),
                    preferred_element_type=F32,
                )
                for p in range(0, wide, 8):
                    n = k + p
                    buf_ref[buf, d, n // 24, n % 24 : n % 24 + 8, :] = res[
                        p : p + 8
                    ].astype(BF)
        for c in copies(slot, buf):
            c.start()

        @pl.when(slot == ROUNDS - 1)
        def _():
            for c in copies(slot - 1, 1 - buf):
                c.wait()
            for c in copies(slot, buf):
                c.wait()


def correlate(meta, stack, table, arrays, out):
    n_arr = len(arrays) // 2
    units = 2 * n_arr
    lanes = 24 * units
    steps = F // FG
    last = steps - 1
    in_specs = [
        pl.BlockSpec((FG, STACK, W2), lambda i, m: (jnp.minimum(i, last), 0, 0)),
        pl.BlockSpec((2 * F, LAGS), lambda i, m: (0, 0)),
    ]
    in_specs += [
        pl.BlockSpec((2, GROUP, W2), lambda i, m: (0, jnp.minimum(i, last), 0))
    ] * (2 * n_arr)
    args = [meta, stack, table] + list(arrays)
    aliases = {}
    if out is not None:
        in_specs.append(pl.BlockSpec(memory_space=pl.ANY))
        aliases = {len(args): 0}
        args.append(out)
    n_tiles = (lanes + 127) // 128
    return pl.pallas_call(
        functools.partial(
            correlate_kernel, n_arr, out is not None, 1.0 / math.sqrt(W)
        ),
        grid_spec=pltpu.PrefetchScalarGridSpec(
            num_scalar_prefetch=1,
            grid=(steps + ROUNDS,),
            in_specs=in_specs,
            out_specs=pl.BlockSpec(memory_space=pl.ANY),
            scratch_shapes=[
                pltpu.VMEM((n_tiles, STACK * F, 128), F32),
                pltpu.VMEM((2, CH, units, 24, LAGS), BF),
                pltpu.SemaphoreType.DMA((2, units)),
            ],
        ),
        out_shape=jax.ShapeDtypeStruct((ROUNDS, CH, UNITS, 24, LAGS), BF),
        input_output_aliases=aliases,
        compiler_params=pltpu.CompilerParams(vmem_limit_bytes=48 << 20),
        cost_estimate=pl.CostEstimate(
            flops=2 * F * STACK * W2 * lanes,
            bytes_accessed=2 * F * W2 * (STACK + lanes) + 2 * 84 * lanes * LAGS,
            transcendentals=0,
        ),
        name="correlate",
    )(*args)


def lag_table():
    freq_index = jnp.arange(F, dtype=jnp.int32)
    lag_index = jnp.arange(LAGS, dtype=jnp.int32)
    product = freq_index[:, None] * lag_index[None, :] % LAGS
    phase = product.astype(F32) * (2.0 * math.pi / LAGS)
    weight = 1.0 / math.sqrt(F)
    pair = jnp.stack([jnp.cos(phase), -jnp.sin(phase)]) * weight
    return pair.astype(BF).reshape(2 * F, LAGS)


def shift_plane(value, first, step):
    pairs = []
    for core in range(2):
        for y in range(4):
            for x in range(4):
                if (core == 0) == first:
                    ty, tx = y, (x + step) % 4
                else:
                    ty, tx = (y + step) % 4, x
                pairs.append((core * 16 + y * 4 + x, core * 16 + ty * 4 + tx))
    return lax.ppermute(value, ("core", "y", "x"), pairs)


def shift_axis(value, axis, size, step):
    return lax.ppermute(value, axis, [(i, (i + step) % size) for i in range(size)])


def shards(spectra):
    core, zh = lax.axis_index("core"), lax.axis_index("zh")
    y, x, zl = lax.axis_index("y"), lax.axis_index("x"), lax.axis_index("zl")
    half = ROWS // 2
    own = whiten(spectra)

    group = zh * 2 + core
    slot_groups = []
    for dz, other in ((0, 1), (3, 0), (3, 1), (1, 0), (1, 1), (2, 0), (2, 1)):
        slot_groups.append(((zh + dz) % 4) * 2 + (core + other) % 2)
    partner = jnp.stack(slot_groups)
    last = 2 * 4 - 1
    slot_rounds = jnp.where(
        group == last,
        partner,
        jnp.where(partner == last, group, ((group + partner) * 4) % last),
    )

    def unit(p, q):
        dy = jnp.where(core == 0, q, p)
        dx = jnp.where(core == 0, p, q)
        return ((y + dy) % 4) * 4 + (x + dx) % 4

    def meta(pairs):
        units = jnp.stack([unit(p, q) for p, q in pairs])
        head = jnp.concatenate([zl.reshape(1), slot_rounds, units])
        return head.astype(jnp.int32)

    other = shift_axis(own, "zl", 2, 1)
    table = lag_table()

    def along_first(block):
        left = shift_plane(block, True, 1)
        right = shift_plane(block, True, -1)
        lower = shift_plane(left[:half], True, 1)
        upper = shift_plane(right[half:], True, -1)
        near = jnp.concatenate([block, left], 0)
        far = jnp.concatenate([right, lower, upper], 0)
        return near, far

    def view(a):
        return a.reshape(2, ROWS, W2)

    lines = [along_first(own), along_first(other)]

    zm = shift_axis(own, "zh", 4, 1)
    zp = shift_axis(own, "zh", 4, -1)
    zo_low = shift_axis(zm[:half], "zh", 4, 1)
    zo_high = shift_axis(zp[half:], "zh", 4, -1)
    zo = jnp.concatenate([zo_low, zo_high], 0)
    cross = [shift_axis(v, "core", 2, 1) for v in (own, zm, zp, zo)]
    stack = make_stack([cross[0], zm, cross[1], zp, cross[2], zo, cross[3]])

    sides, facing = [], []
    for near, far in lines:
        a_near = shift_plane(near, False, 1)
        a_far = shift_plane(far, False, 1)
        b_near = shift_plane(near, False, -1)
        b_far = shift_plane(far, False, -1)
        o_near = shift_plane(a_near, False, 1)
        o_far = shift_plane(b_far, False, -1)
        sides.append([a_near, a_far, b_near, b_far])
        facing.append([o_near, o_far])

    def weave(pair):
        return [view(v) for both in zip(*pair) for v in both]

    line_units = [(0, 0), (-1, 0), (1, 0), (2, 0)]
    out = correlate(meta(line_units), stack, table, weave(lines), None)
    side_units = [(p, q) for q in (-1, 1) for p, _ in line_units]
    out = correlate(meta(side_units), stack, table, weave(sides), out)
    far_units = [(p, 2) for p, _ in line_units]
    out = correlate(meta(far_units), stack, table, weave(facing), out)
    out = out.reshape(ROUNDS, CH, UNITS * 24, LAGS)
    out = jnp.transpose(out, (0, 2, 1, 3))
    return out.reshape(ROUNDS, 1, UNITS * 24, 1, CH, LAGS)


def solution(mesh):
    axes = ("zh", "core", "y", "x", "zl")
    fine = Mesh(mesh.devices.reshape(4, 2, 4, 4, 2), axes)
    return jax.shard_map(
        shards,
        mesh=fine,
        in_specs=(P(axes, None, None),),
        out_specs=P(None, axes[:2], None, axes[2:], None, None),
        check_vma=False,
    )
```

```python
import functools
import math

import jax
import jax.numpy as jnp
from jax import lax
from jax.experimental import pallas as pl
from jax.experimental.pallas import tpu as pltpu
from jax.sharding import Mesh, PartitionSpec as P


BF = jnp.bfloat16
F32 = jnp.float32
F, W, CH, LAGS = 64, 192, 12, 128
W2 = 2 * W
ROWS = F * CH
ROUNDS = 7
BG = 16
FG = 4
UNROLL = 4
DB = 4
PITCH = 68
GROUP = FG * CH
UNITS = 16
STACK = ROUNDS * 2 * CH


def whiten_kernel(x_ref, o_ref, t_ref):
    for c in range(CH):
        v = x_ref[c].astype(F32)
        total = jnp.sum(v * v, axis=0, keepdims=True)
        mean = (total[:, :W] + total[:, W:]) * (1.0 / F)
        amplitude = jnp.sqrt(mean + 1e-06)
        divisor = jnp.concatenate([amplitude, amplitude], 1)
        q = v / divisor
        for j in range(3):
            t_ref[j, pl.ds(c, F, stride=CH), :] = q[:, 128 * j : 128 * j + 128]
    for j in range(3):
        o_ref[:, 128 * j : 128 * j + 128] = t_ref[j].astype(BF)


def whiten(spectra):
    return pl.pallas_call(
        whiten_kernel,
        out_shape=jax.ShapeDtypeStruct((ROWS, W2), BF),
        scratch_shapes=[pltpu.VMEM((3, ROWS, 128), F32)],
        cost_estimate=pl.CostEstimate(
            flops=6 * ROWS * W2, bytes_accessed=4 * ROWS * W2, transcendentals=0
        ),
        name="whiten",
    )(spectra)


def stack_kernel(*refs):
    o_ref = refs[-1]

    def group(t, carry):
        plain, turned = [], []
        for ref in refs[:-1]:
            v = ref[pl.ds(pl.multiple_of(t * GROUP, GROUP), GROUP), :].astype(F32)
            plain.append(v)
            turned.append(jnp.concatenate([-v[:, W:], v[:, :W]], 1))
        for j in range(FG):
            rows = slice(CH * j, CH * j + CH)
            parts = []
            for v, r in zip(plain, turned):
                parts += [v[rows], r[rows]]
            o_ref[t * FG + j] = jnp.concatenate(parts, 0).astype(BF)
        return carry

    lax.fori_loop(0, BG // FG, group, 0, unroll=UNROLL)


def make_stack(blocks):
    return pl.pallas_call(
        stack_kernel,
        grid=(F // BG,),
        in_specs=[pl.BlockSpec((BG * CH, W2), lambda i: (i, 0))] * ROUNDS,
        out_specs=pl.BlockSpec((BG, STACK, W2), lambda i: (i, 0, 0)),
        compiler_params=pltpu.CompilerParams(vmem_limit_bytes=48 << 20),
        out_shape=jax.ShapeDtypeStruct((F, STACK, W2), BF),
        cost_estimate=pl.CostEstimate(
            flops=2 * F * STACK * W2,
            bytes_accessed=3 * F * STACK * W2,
            transcendentals=0,
        ),
        name="partners",
    )(*blocks)


def correlate_kernel(n_arr, aliased, scale, *refs):
    meta = refs[0]
    stack_ref, table_ref = refs[1], refs[2]
    row_refs = refs[3 : 3 + 2 * n_arr]
    at = 3 + 2 * n_arr + (1 if aliased else 0)
    out_ref, spec_ref, buf_ref, sem = refs[at : at + 4]
    units = 2 * n_arr
    lanes = 24 * units
    i = pl.program_id(0)
    swap = meta[0] == 1

    def group(t, carry):
        at_rows = pl.ds(pl.multiple_of(t * GROUP, GROUP), GROUP)
        firsts, seconds = [], []
        for a in range(n_arr):
            for b in range(2):
                u = row_refs[2 * a][b, at_rows, :].astype(F32)
                v = row_refs[2 * a + 1][b, at_rows, :].astype(F32)
                firsts.append(jnp.where(swap, v, u))
                seconds.append(jnp.where(swap, u, v))
        for j in range(FG):
            rows = slice(CH * j, CH * j + CH)
            parts = []
            for u, v in zip(firsts, seconds):
                parts += [u[rows], v[rows]]
            mat = jnp.concatenate(parts, 0).astype(BF)
            f = t * FG + j
            res = (
                lax.dot_general(
                    stack_ref[f],
                    mat,
                    (((1,), (1,)), ((), ())),
                    preferred_element_type=F32,
                )
                * scale
            )
            for k in range(0, lanes, 128):
                wide = min(128, lanes - k)
                spec_ref[
                    k // 128, pl.ds(i * BG + f, STACK, stride=PITCH), 0:wide
                ] = res[:, k : k + wide]
        return carry

    lax.fori_loop(0, BG // FG, group, 0, unroll=UNROLL)

    def copies(slot):
        return [
            pltpu.make_async_copy(
                buf_ref.at[slot, :, k],
                out_ref.at[meta[1 + slot], :, meta[8 + k]],
                sem.at[slot, k],
            )
            for k in range(units)
        ]

    def finish(slot):
        table = table_ref[...]
        base = slot * (24 * PITCH)
        for k in range(0, lanes, 128):
            wide = min(128, lanes - k)
            for d0 in range(0, CH, DB):
                cross = jnp.concatenate(
                    [
                        jnp.concatenate(
                            [
                                spec_ref[k // 128, pl.ds(base + d * PITCH, F), :],
                                spec_ref[k // 128, pl.ds(base + (CH + d) * PITCH, F), :],
                            ],
                            0,
                        ).astype(BF)
                        for d in range(d0, d0 + DB)
                    ],
                    1,
                )
                res = lax.dot_general(
                    cross,
                    table,
                    (((0,), (0,)), ((), ())),
                    preferred_element_type=F32,
                )
                for d in range(d0, d0 + DB):
                    for p in range(0, wide, 8):
                        n = k + p
                        at = (d - d0) * 128 + p
                        buf_ref[slot, d, n // 24, n % 24 : n % 24 + 8, :] = res[
                            at : at + 8
                        ].astype(BF)

    @pl.when(i == pl.num_programs(0) - 1)
    def _():
        for slot in range(ROUNDS):
            finish(slot)
            for c in copies(slot):
                c.start()
        for slot in range(ROUNDS):
            for c in copies(slot):
                c.wait()


def correlate(meta, stack, table, arrays, out):
    n_arr = len(arrays) // 2
    units = 2 * n_arr
    lanes = 24 * units
    in_specs = [
        pl.BlockSpec((BG, STACK, W2), lambda i, m: (i, 0, 0)),
        pl.BlockSpec((2 * F, LAGS), lambda i, m: (0, 0)),
    ]
    in_specs += [
        pl.BlockSpec((2, BG * CH, W2), lambda i, m: (0, i, 0))
    ] * (2 * n_arr)
    args = [meta, stack, table] + list(arrays)
    aliases = {}
    if out is not None:
        in_specs.append(pl.BlockSpec(memory_space=pl.ANY))
        aliases = {len(args): 0}
        args.append(out)
    n_tiles = (lanes + 127) // 128
    return pl.pallas_call(
        functools.partial(
            correlate_kernel, n_arr, out is not None, 1.0 / math.sqrt(W)
        ),
        grid_spec=pltpu.PrefetchScalarGridSpec(
            num_scalar_prefetch=1,
            grid=(F // BG,),
            in_specs=in_specs,
            out_specs=pl.BlockSpec(memory_space=pl.ANY),
            scratch_shapes=[
                pltpu.VMEM((n_tiles, STACK * PITCH, 128), F32),
                pltpu.VMEM((ROUNDS, CH, units, 24, LAGS), BF),
                pltpu.SemaphoreType.DMA((ROUNDS, units)),
            ],
        ),
        out_shape=jax.ShapeDtypeStruct((ROUNDS, CH, UNITS, 24, LAGS), BF),
        input_output_aliases=aliases,
        compiler_params=pltpu.CompilerParams(vmem_limit_bytes=48 << 20),
        cost_estimate=pl.CostEstimate(
            flops=2 * F * STACK * W2 * lanes,
            bytes_accessed=2 * F * W2 * (STACK + lanes) + 2 * 84 * lanes * LAGS,
            transcendentals=0,
        ),
    )(*args)


def lag_table():
    freq_index = jnp.arange(F, dtype=jnp.int32)
    lag_index = jnp.arange(LAGS, dtype=jnp.int32)
    product = freq_index[:, None] * lag_index[None, :] % LAGS
    phase = product.astype(F32) * (2.0 * math.pi / LAGS)
    weight = 1.0 / math.sqrt(F)
    pair = jnp.stack([jnp.cos(phase), -jnp.sin(phase)]) * weight
    return pair.astype(BF).reshape(2 * F, LAGS)


def shift_plane(value, first, step):
    pairs = []
    for core in range(2):
        for y in range(4):
            for x in range(4):
                if (core == 0) == first:
                    ty, tx = y, (x + step) % 4
                else:
                    ty, tx = (y + step) % 4, x
                pairs.append((core * 16 + y * 4 + x, core * 16 + ty * 4 + tx))
    return lax.ppermute(value, ("core", "y", "x"), pairs)


def shift_axis(value, axis, size, step):
    return lax.ppermute(value, axis, [(i, (i + step) % size) for i in range(size)])


def body(spectra):
    core, zh = lax.axis_index("core"), lax.axis_index("zh")
    y, x, zl = lax.axis_index("y"), lax.axis_index("x"), lax.axis_index("zl")
    half = ROWS // 2
    own = whiten(spectra)

    group = zh * 2 + core
    slot_groups = []
    for dz, other in ((0, 1), (3, 0), (3, 1), (1, 0), (1, 1), (2, 0), (2, 1)):
        slot_groups.append(((zh + dz) % 4) * 2 + (core + other) % 2)
    partner = jnp.stack(slot_groups)
    last = 2 * 4 - 1
    slot_rounds = jnp.where(
        group == last,
        partner,
        jnp.where(partner == last, group, ((group + partner) * 4) % last),
    )

    def unit(p, q):
        dy = jnp.where(core == 0, q, p)
        dx = jnp.where(core == 0, p, q)
        return ((y + dy) % 4) * 4 + (x + dx) % 4

    def meta(pairs):
        units = jnp.stack([unit(p, q) for p, q in pairs])
        head = jnp.concatenate([zl.reshape(1), slot_rounds, units])
        return head.astype(jnp.int32)

    other = shift_axis(own, "zl", 2, 1)
    table = lag_table()

    def along_first(block):
        left = shift_plane(block, True, 1)
        right = shift_plane(block, True, -1)
        across = shift_plane(right, True, -1)
        near = jnp.concatenate([block, left], 0)
        far = jnp.concatenate([right, across], 0)
        return near, far

    def view(a):
        return a.reshape(2, ROWS, W2)

    lines = [along_first(own), along_first(other)]

    zm = shift_axis(own, "zh", 4, 1)
    zp = shift_axis(own, "zh", 4, -1)
    zo_low = shift_axis(zm[:half], "zh", 4, 1)
    zo_high = shift_axis(zp[half:], "zh", 4, -1)
    zo = jnp.concatenate([zo_low, zo_high], 0)
    cross = [shift_axis(v, "core", 2, 1) for v in (own, zm, zp, zo)]
    stack = make_stack([cross[0], zm, cross[1], zp, cross[2], zo, cross[3]])

    sides, facing = [], []
    for tag, (near, far) in zip("01", lines):
        a_near = shift_plane(near, False, 1)
        if tag == "0":
            b_near = shift_plane(near, False, -1)
        else:
            b_near = shift_axis(sides[0][2], "zl", 2, 1)
        a_far = shift_plane(far, False, 1)
        b_far = shift_plane(far, False, -1)
        o_near = shift_plane(a_near, False, 1)
        o_far = shift_plane(b_far, False, -1)
        sides.append([a_near, a_far, b_near, b_far])
        facing.append([o_near, o_far])

    def weave(pair):
        return [view(v) for both in zip(*pair) for v in both]

    line_units = [(0, 0), (-1, 0), (1, 0), (2, 0)]
    out = correlate(meta(line_units), stack, table, weave(lines), None)
    side_units = [(p, q) for q in (-1, 1) for p, _ in line_units]
    out = correlate(meta(side_units), stack, table, weave(sides), out)
    far_units = [(p, 2) for p, _ in line_units]
    out = correlate(meta(far_units), stack, table, weave(facing), out)
    out = out.reshape(ROUNDS, CH, UNITS * 24, LAGS)
    out = jnp.transpose(out, (0, 2, 1, 3))
    return out.reshape(ROUNDS, 1, UNITS * 24, 1, CH, LAGS)


def solution(mesh):
    axes = ("zh", "core", "y", "x", "zl")
    fine = Mesh(mesh.devices.reshape(4, 2, 4, 4, 2), axes)
    return jax.shard_map(
        body,
        mesh=fine,
        in_specs=(P(axes, None, None),),
        out_specs=P(None, axes[:2], None, axes[2:], None, None),
        check_vma=False,
    )
```
